32 devices in a mesh: group: 2 (over x), ctx: 16 (over z, y, core).
Axes of the slice: x: 2, y: 2, z: 4, core: 2. Of those that a mesh axis runs over, the one named last changes fastest.
Arguments:
- normed_hidden: bfloat16 [4096, 8192], P(('group', 'ctx')), parts along dimension 0, may hold values from -6 to 6
- queries: bfloat16 [4096, 4096], P(('group', 'ctx')), parts along dimension 0, may hold values from -45 to 45
- keys: bfloat16 [4096, 512], P(('group', 'ctx')), parts along dimension 0, may hold values from -6 to 6
- value_frozen_matrix: bfloat16 [8192, 512], P('ctx'), may hold values from -0.0625 to 0.0625
- adapter_down_weight: bfloat16 [8192, 64], replicated, may hold values from -0.0625 to 0.0625
- adapter_up_weight: bfloat16 [64, 512], replicated, may hold values from -0.75 to 0.75
- block_slot_index: int32 [64], P(('group', 'ctx')), parts along dimension 0, may hold values from 0 to 31, each once
Outputs:
- attended: bfloat16 [4096, 4096], P(('group', 'ctx')), parts along dimension 0
The draws below stay inside these ranges and needn't reach their ends.
There are 2 independent parts, one for each index of `group`. The reference program is written for one: setup_inputs(seed, part) draws one part's arguments, and reference() takes and returns one part's arrays. A program takes and returns all parts, laid end to end along the dimension named above; an argument that names none is the same for every part. Nothing has to cross between parts.
Inputs may be any that keep to these rules, and one draw needn't show every extreme that they name: `block_slot_index`: each of the 32 blocks is named once; slot j holds rows j*64 to (j+1)*64 - 1.
All inputs are finite; a program needn't handle non-finite values.
Results may differ from the reference program's by a relative error of at most 0.0054.
Values may be sent and summed in bfloat16 or wider, within the bound.
No kernel may reach another device: no remote copies, remote signals or barrier semaphores. Data moves between devices by JAX's collectives and lax.ppermute only.
A program may use at most 192 MiB of HBM per device.

```python
import jax
import jax.numpy as jnp
from jax import lax

MODEL_WIDTH = 8192
QH = 32
KVH = 4
HD = 128
ADAPTER_RANK = 64
TOK_DEV = 128
BLK = 64
SEQ = 2048
NBLK = 32
G = 8
KEY_VALUE_WIDTH = 512
QW = 4096


def shared_fields(key):
    base_key = jax.random.fold_in(key, 11)
    key_a = jax.random.fold_in(base_key, 0)
    key_b = jax.random.fold_in(base_key, 1)
    key_d = jax.random.fold_in(base_key, 3)
    key_e = jax.random.fold_in(base_key, 4)
    base_q = jnp.clip(jax.random.normal(key_a, (SEQ, QH * HD), jnp.float32) * 2.5, -15.0, 15.0)
    base_k = jnp.clip(jax.random.normal(key_b, (SEQ, KVH * HD), jnp.float32), -6.0, 6.0)
    picked = jnp.zeros((SEQ,), dtype=bool)
    strength = jax.random.uniform(key_d, (SEQ, 1), jnp.float32, 8.0, 24.0)
    shrink = jax.random.uniform(key_e, (SEQ, 1), jnp.float32, 0.004, 0.012)
    repeated = jnp.repeat(base_k.reshape(SEQ, KVH, HD), QH // KVH, axis=1).reshape(SEQ, QH * HD)
    queries = jnp.where(picked[:, None], strength * repeated, base_q)
    next_k = jnp.roll(base_k, -1, axis=0)
    next_pick = jnp.roll(picked, -1)
    next_shrink = jnp.roll(shrink, -1, axis=0)
    keys = jnp.where(next_pick[:, None], next_k * (1.0 - next_shrink), base_k)
    return (queries, keys)


def draw_queries(key, part):
    return shared_fields(key)[0].astype(jnp.bfloat16)


def draw_keys(key, part):
    return shared_fields(key)[1].astype(jnp.bfloat16)


def block_scale(own_key, extent, cuts, least, largest):
    factor_of = 1.0
    for dim, parts in cuts:
        draws = jax.random.uniform(jax.random.fold_in(jax.random.fold_in(own_key, 6), dim), (parts,), jnp.float32, least / len(cuts), largest / len(cuts))
        factor_of = factor_of * jnp.repeat(jnp.exp(draws), extent[dim] // parts).reshape((-1,) + (1,) * (len(extent) - 1 - dim))
    return factor_of


def gaussian(rng, extent, width, reach, shards=(), kind=jnp.bfloat16):
    values = jax.random.normal(rng, extent, jnp.float32) * width
    if len(shards) > 0:
        values = block_scale(rng, extent, shards, -0.22, 0.18) * values
    return jnp.clip(values, min=-reach, max=reach).astype(kind)


def setup_inputs(seed: int = 0, part: int = 0) -> dict:
    streams_of = jax.random.split(jax.random.key(seed), 8)
    part_splits = jax.random.split(jax.random.fold_in(streams_of[7], part), 8)
    normed_hidden = gaussian(part_splits[0], (SEQ, MODEL_WIDTH), 1.0, 6.0, ((0, 16),))
    queries = draw_queries(jax.random.fold_in(jax.random.fold_in(streams_of[7], part), 71), part)
    keys = draw_keys(jax.random.fold_in(jax.random.fold_in(streams_of[7], part), 71), part)
    value_frozen_matrix = gaussian(streams_of[3], (MODEL_WIDTH, KEY_VALUE_WIDTH), MODEL_WIDTH ** -0.5, 0.0625, ((0, 16),))
    adapter_down_weight = gaussian(streams_of[4], (MODEL_WIDTH, ADAPTER_RANK), MODEL_WIDTH ** -0.5, 0.0625)
    adapter_up_weight = gaussian(streams_of[5], (ADAPTER_RANK, KEY_VALUE_WIDTH), ADAPTER_RANK ** -0.5, 0.75)
    block_slot_index = jax.random.permutation(part_splits[6], NBLK).astype(jnp.int32)
    return {"normed_hidden": normed_hidden, "queries": queries, "keys": keys, "value_frozen_matrix": value_frozen_matrix, "adapter_down_weight": adapter_down_weight, "adapter_up_weight": adapter_up_weight, "block_slot_index": block_slot_index}


def reference(normed_hidden, queries, keys, value_frozen_matrix, adapter_down_weight, adapter_up_weight, block_slot_index):
    offsets = jnp.arange(BLK, dtype=jnp.int32)
    positions = (block_slot_index[:, None].astype(jnp.int32) * BLK + offsets[None, :]).reshape(SEQ)
    frozen_output = jnp.dot(normed_hidden, value_frozen_matrix, preferred_element_type=jnp.float32)
    low_rank_output = jnp.dot(normed_hidden, adapter_down_weight, preferred_element_type=jnp.float32).astype(jnp.bfloat16)
    value_output = (frozen_output + 0.5 * jnp.dot(low_rank_output, adapter_up_weight, preferred_element_type=jnp.float32)).astype(jnp.bfloat16)
    keys_f = keys.astype(jnp.float32).reshape(SEQ, KVH, HD)
    values_f = value_output.astype(jnp.float32).reshape(SEQ, KVH, HD)
    scale = 1.0 / (HD ** 0.5)
    count = SEQ // TOK_DEV
    q_blocks = queries.reshape(count, TOK_DEV, QW)
    p_blocks = positions.reshape(count, TOK_DEV)

    def one_block(pair):
        q_blk, q_pos = pair
        q_f = q_blk.astype(jnp.float32).reshape(TOK_DEV, KVH, G, HD)
        scores = jnp.einsum("tkgd,skd->kgts", q_f, keys_f) * scale
        visible = (q_pos[:, None] >= positions[None, :])[None, None]
        scores = jnp.where(visible, scores, -1e30)
        top = jnp.max(scores, axis=-1, keepdims=True)
        weights = jnp.where(visible, jnp.exp(scores - top), 0.0)
        total = jnp.sum(weights, axis=-1)
        rounded = lax.optimization_barrier(weights.astype(jnp.bfloat16))
        summed = jnp.einsum("kgts,skd->kgtd", rounded.astype(jnp.float32), values_f)
        result = summed / total[..., None]
        return jnp.transpose(result, (2, 0, 1, 3)).reshape(TOK_DEV, QW).astype(jnp.bfloat16)

    return lax.map(one_block, (q_blocks, p_blocks)).reshape(SEQ, QW)
```

```python
import functools

import jax
import jax.numpy as jnp
from jax import lax
from jax.experimental import pallas as pl
from jax.experimental.pallas import tpu as pltpu
from jax.sharding import PartitionSpec as P

QH = 32
KVH = 4
HD = 128
BLK = 64


def shards(
    normed_hidden,
    queries,
    keys,
    value_frozen_matrix,
    adapter_down_weight,
    adapter_up_weight,
    block_slot_index,
):
    tokens = normed_hidden.shape[0]
    scale = 1.0 / HD**0.5
    offsets = jnp.arange(BLK, dtype=jnp.int32)
    table = lax.all_gather(block_slot_index, "ctx", axis=0, tiled=True)
    my_pos = (block_slot_index[:, None] * BLK + offsets[None, :]).reshape(tokens)
    frozen_output = jnp.dot(
        normed_hidden,
        lax.all_gather(value_frozen_matrix, "ctx", axis=0, tiled=True),
        preferred_element_type=jnp.float32,
    )
    low_rank_output = jnp.dot(
        normed_hidden, adapter_down_weight, preferred_element_type=jnp.float32
    ).astype(jnp.bfloat16)
    value_output = (
        frozen_output
        + 0.5 * jnp.dot(low_rank_output, adapter_up_weight, preferred_element_type=jnp.float32)
    ).astype(jnp.bfloat16)
    slots_here = tokens // BLK
    query_slots = [
        queries[which * BLK : (which + 1) * BLK].reshape(BLK, KVH, QH // KVH, HD)
        for which in range(slots_here)
    ]
    pos_slots = [my_pos[which * BLK : (which + 1) * BLK] for which in range(slots_here)]
    shape_stat = (KVH, QH // KVH, BLK)
    init = tuple(
        (
            (
                jnp.full(shape_stat, -1e30, jnp.float32),
                jnp.zeros(shape_stat, jnp.float32),
                jnp.zeros(shape_stat + (HD,), jnp.float32),
            )
            for which in range(slots_here)
        )
    )
    key_piece = lax.all_gather(keys, "ctx", axis=0, tiled=True)
    count = key_piece.shape[0]
    key_pos = (table[:, None] * BLK + offsets[None, :]).reshape(count)
    key_three = key_piece.reshape(count, KVH, HD)
    value_three = lax.all_gather(value_output, "ctx", axis=0, tiled=True).reshape(count, KVH, HD)
    lowest_key = jnp.min(key_pos)
    updated = []
    for attend_which in range(slots_here):
        q_part = query_slots[attend_which]
        q_pos = pos_slots[attend_which]

        def update(state, q_part=q_part, q_pos=q_pos):
            top, total, accum = state
            scores = (
                jnp.einsum("tkgd,skd->kgts", q_part, key_three, preferred_element_type=jnp.float32)
                * scale
            )
            visible = (q_pos[:, None] >= key_pos[None, :])[None, None]
            scores = jnp.where(visible, scores, -1e30)
            top_new = jnp.maximum(top, jnp.max(scores, axis=-1))
            weights = jnp.where(visible, jnp.exp(scores - top_new[..., None]), 0.0)
            total = jnp.sum(weights, axis=-1)
            accum = jnp.einsum(
                "kgts,skd->kgtd",
                weights.astype(jnp.bfloat16),
                value_three,
                preferred_element_type=jnp.float32,
            )
            return (top_new, total, accum)

        def keep(state):
            return state

        updated.append(lax.cond(lowest_key <= jnp.max(q_pos), update, keep, init[attend_which]))
    states = tuple(updated)
    outputs = []
    for which in range(slots_here):
        result = states[which][2] / states[which][1][..., None]
        outputs.append(
            jnp.transpose(result, (2, 0, 1, 3)).reshape(BLK, QH * HD).astype(jnp.bfloat16)
        )
    return jnp.concatenate(outputs, axis=0)


PARTS = 2
NZ = 4
NY = 2
NCORE = 2
CHIPS = NZ * NY
AXES = ("group", "ctx")
LANES = 128


def device(g, z, y, c):
    return ((g * NZ + z) * NY + y) * NCORE + c


def pairs(move):
    return [
        (device(g, z, y, c), device(*move(g, z, y, c)))
        for g in range(PARTS)
        for z in range(NZ)
        for y in range(NY)
        for c in range(NCORE)
    ]


TO_CORE = pairs(lambda g, z, y, c: (g, z, y, c ^ 1))
TO_X = pairs(lambda g, z, y, c: (g ^ 1, z, y, c))
TO_Y = pairs(lambda g, z, y, c: (g, z, y ^ 1, c))
TO_Z = [pairs(lambda g, z, y, c, k=k: (g, z ^ k, y, c)) for k in range(NZ)]


def send(x, where):
    return lax.ppermute(x, AXES, where)


def split_kernel(half_ref, x_ref, mine_ref, other_ref, *, shards_of, part):
    g = half_ref[0]
    for s in range(shards_of):
        low = s * PARTS * part
        to = pl.ds(s * part, part)
        mine_ref[:, to] = x_ref[:, pl.ds(pl.multiple_of(low + g * part, part), part)]
        other_ref[:, to] = x_ref[:, pl.ds(pl.multiple_of(low + (1 - g) * part, part), part)]


def split_columns(g, x, shards_of):
    rows, width = x.shape
    part = width // shards_of // PARTS
    half = jax.ShapeDtypeStruct((rows, width // PARTS), x.dtype)
    return pl.pallas_call(
        functools.partial(split_kernel, shards_of=shards_of, part=part),
        out_shape=(half, half),
        in_specs=[pl.BlockSpec(memory_space=pltpu.SMEM), pl.BlockSpec(memory_space=pltpu.VMEM)],
        out_specs=(pl.BlockSpec(memory_space=pltpu.VMEM),) * 2,
        cost_estimate=pl.CostEstimate(flops=0, bytes_accessed=4 * x.size, transcendentals=0),
        name="split_columns",
    )(g, x)


def value_kernel(shard_ref, *refs, count, part, has_init):
    xs, ws = refs[:2], refs[2 : 2 + count]
    out = refs[-1]
    rows = xs[0].shape[0]
    for t in range(2):
        total = refs[2 + count][t * rows : (t + 1) * rows, :] if has_init else None
        for k in range(count):
            for which in range(NCORE):
                at = pl.multiple_of(shard_ref[k * NCORE + which] * part, part)
                term = jnp.dot(
                    xs[t][:, pl.ds(at, part)],
                    ws[k][which * part : (which + 1) * part, :],
                    preferred_element_type=jnp.float32,
                )
                total = term if total is None else total + term
        out[t * rows : (t + 1) * rows, :] = total


def value_product(shard_of, xs, ws, init=None):
    rows = xs[0].shape[0]
    part = ws[0].shape[0] // NCORE
    width = ws[0].shape[1]
    extra = [] if init is None else [init]
    vmem = pl.BlockSpec(memory_space=pltpu.VMEM)
    return pl.pallas_call(
        functools.partial(
            value_kernel, count=len(ws), part=part, has_init=init is not None
        ),
        out_shape=jax.ShapeDtypeStruct((2 * rows, width), jnp.float32),
        in_specs=[pl.BlockSpec(memory_space=pltpu.SMEM)] + [vmem] * (2 + len(ws) + len(extra)),
        out_specs=vmem,
        cost_estimate=pl.CostEstimate(
            flops=4 * rows * len(ws) * 2 * part * width,
            bytes_accessed=4 * xs[0].size + 2 * len(ws) * ws[0].size,
            transcendentals=0,
        ),
        name="value_product",
    )(shard_of, *xs, *ws, *extra)


def weight_kernel(qid_ref, q_ref, kpos_ref, *refs, count, rows_of, heads, lane):
    ks = refs[:count]
    p_ref, total_ref, s_ref, bias_ref = refs[count:]
    i = pl.program_id(0)
    keys_of = rows_of
    q = jnp.concatenate([q_ref[:, j * HD : (j + 1) * HD] for j in range(heads)], axis=0)
    for k in range(count):
        s_ref[:, k * keys_of : (k + 1) * keys_of] = lax.dot_general(
            q,
            ks[k][:rows_of, lane : lane + HD],
            (((1,), (1,)), ((), ())),
            preferred_element_type=jnp.float32,
        )
    qpos = qid_ref[i] * BLK + lax.broadcasted_iota(jnp.int32, bias_ref.shape, 0)
    bias_ref[...] = jnp.where(qpos >= kpos_ref[...], 0.0, -1e30)
    factor = 1.4426950408889634 / HD**0.5
    tile = 16

    def some(r, _):
        at = pl.multiple_of(r * tile, tile)
        row = pl.multiple_of(lax.rem(r, BLK // tile) * tile, tile)
        s = s_ref[pl.ds(at, tile), :] * factor + bias_ref[pl.ds(row, tile), :]
        e = jnp.exp2(s - jnp.max(s, axis=1, keepdims=True))
        p_ref[pl.ds(at, tile), :] = e.astype(jnp.bfloat16)
        total_ref[pl.ds(at, tile), :] = jnp.broadcast_to(
            jnp.sum(e, axis=1, keepdims=True), (tile, LANES)
        )
        return 0

    lax.fori_loop(0, heads * BLK // tile, some, 0, unroll=2)


def weights_of(qid, q, kpos, chunks, rows_of, head):
    tokens = q.shape[0]
    heads = QH // KVH
    rows = heads * BLK
    count = len(chunks)
    keys = count * rows_of
    blocks = tokens // BLK
    whole = lambda i: (0, 0)
    return pl.pallas_call(
        functools.partial(
            weight_kernel, count=count, rows_of=rows_of, heads=heads, lane=head * HD
        ),
        grid=(blocks,),
        out_shape=(
            jax.ShapeDtypeStruct((blocks * rows, keys), jnp.bfloat16),
            jax.ShapeDtypeStruct((blocks * rows, LANES), jnp.float32),
        ),
        in_specs=[
            pl.BlockSpec(memory_space=pltpu.SMEM),
            pl.BlockSpec((BLK, heads * HD), lambda i: (i, head)),
            pl.BlockSpec((1, keys), whole),
        ]
        + [pl.BlockSpec(chunks[0].shape, whole)] * count,
        out_specs=(
            pl.BlockSpec((rows, keys), lambda i: (i, 0)),
            pl.BlockSpec((rows, LANES), lambda i: (i, 0)),
        ),
        scratch_shapes=[
            pltpu.VMEM((rows, keys), jnp.float32),
            pltpu.VMEM((BLK, keys), jnp.float32),
        ],
        cost_estimate=pl.CostEstimate(
            flops=2 * blocks * rows * keys * HD * 4,
            bytes_accessed=2 * blocks * rows * keys,
            transcendentals=blocks * rows * keys,
        ),
        name="weights_of",
    )(qid, q, kpos, *chunks)


def first_kernel(p_ref, *refs, lane):
    vs, out_ref = refs[:-1], refs[-1]
    rows_of = vs[0].shape[0]
    total = None
    for k, v in enumerate(vs):
        term = jnp.dot(
            p_ref[:, k * rows_of : (k + 1) * rows_of],
            v[:, lane : lane + HD],
            preferred_element_type=jnp.float32,
        )
        total = term if total is None else total + term
    out_ref[...] = total


def first_sum(p, vs, head):
    rows = QH // KVH * BLK
    blocks = p.shape[0] // rows
    half = len(vs) * vs[0].shape[0]
    return pl.pallas_call(
        functools.partial(first_kernel, lane=head * HD),
        grid=(blocks,),
        out_shape=jax.ShapeDtypeStruct((blocks * rows, HD), jnp.float32),
        in_specs=[pl.BlockSpec((rows, half), lambda i: (i, 0))]
        + [pl.BlockSpec(vs[0].shape, lambda i: (0, 0))] * len(vs),
        out_specs=pl.BlockSpec((rows, HD), lambda i: (i, 0)),
        cost_estimate=pl.CostEstimate(
            flops=2 * blocks * rows * half * HD,
            bytes_accessed=2 * blocks * rows * half,
            transcendentals=0,
        ),
        name="first_sum",
    )(p, *vs)


def last_kernel(*refs, kv):
    ps, sums, totals = refs[:kv], refs[kv : 2 * kv], refs[2 * kv : 3 * kv]
    vs, out_ref = refs[3 * kv : -1], refs[-1]
    rows_of = vs[0].shape[0]
    heads = QH // KVH
    for h in range(kv):
        total = sums[h][...]
        for k, v in enumerate(vs):
            total = total + jnp.dot(
                ps[h][:, k * rows_of : (k + 1) * rows_of],
                v[:, h * HD : (h + 1) * HD],
                preferred_element_type=jnp.float32,
            )
        result = (total / totals[h][...]).astype(jnp.bfloat16)
        for j in range(heads):
            at = (h * heads + j) * HD
            out_ref[:, at : at + HD] = result[j * BLK : (j + 1) * BLK, :]


def last_sum(ps, sums, totals, vs, first, blocks):
    kv = len(ps)
    rows = QH // KVH * BLK
    half = len(vs) * vs[0].shape[0]
    place = lambda i: (first + i, 0)
    return pl.pallas_call(
        functools.partial(last_kernel, kv=kv),
        grid=(blocks,),
        out_shape=jax.ShapeDtypeStruct((blocks * BLK, kv * QH // KVH * HD), jnp.bfloat16),
        in_specs=[pl.BlockSpec((rows, half), lambda i: (first + i, 1))] * kv
        + [pl.BlockSpec((rows, HD), place)] * kv
        + [pl.BlockSpec((rows, LANES), place)] * kv
        + [pl.BlockSpec(vs[0].shape, lambda i: (0, 0))] * len(vs),
        out_specs=pl.BlockSpec((BLK, kv * QH // KVH * HD), lambda i: (i, 0)),
        cost_estimate=pl.CostEstimate(
            flops=2 * kv * blocks * rows * half * HD,
            bytes_accessed=2 * kv * blocks * rows * half,
            transcendentals=0,
        ),
        name="last_sum",
    )(*ps, *sums, *totals, *vs)


def chip_shards(
    normed_hidden,
    queries,
    keys,
    value_frozen_matrix,
    adapter_down_weight,
    adapter_up_weight,
    block_slot_index,
):
    tokens, model = normed_hidden.shape
    width = keys.shape[1]
    wide = width // NCORE
    qwide = queries.shape[1] // NCORE
    depth = value_frozen_matrix.shape[0]
    part = depth // PARTS
    slots = block_slot_index.shape[0]
    g = lax.axis_index("group")
    here = lax.axis_index("ctx")
    c = here % NCORE
    y = (here // NCORE) % NY
    z = here // (NCORE * NY)

    def columns(x, which, size):
        return lax.dynamic_slice_in_dim(x, which * size, size, axis=1)

    rows_w = lax.dynamic_slice_in_dim(value_frozen_matrix, g * part, part, axis=0)
    ids = block_slot_index.astype(jnp.bfloat16)
    id_rows = jnp.zeros((16, wide), jnp.bfloat16).at[:, :slots].set(ids[None, :])
    core_out = jnp.concatenate(
        [columns(rows_w, 1 - c, wide), columns(keys, 1 - c, wide), id_rows], axis=0
    )
    core_in = send(core_out, TO_CORE)
    w_chunk = jnp.concatenate([columns(rows_w, c, wide), core_in[:part]], axis=0)
    w_line = [w_chunk] + [send(w_chunk, TO_Z[k]) for k in range(1, NZ)]
    w_across = [send(x, TO_Y) for x in w_line]

    x_mine, x_other = split_columns(jnp.reshape(g, (1,)).astype(jnp.int32), normed_hidden, CHIPS * NCORE)
    x_far = send(x_other, TO_X)
    x_partner = send(x_mine, TO_CORE)
    x_far_partner = send(x_far, TO_CORE)

    id_all = jnp.concatenate(
        [id_rows[:, :slots], core_in[part + tokens :, :slots]], axis=1
    )
    id_tail = jnp.zeros((16, wide), jnp.bfloat16).at[:, : 2 * slots].set(id_all)
    k_chunk = jnp.concatenate(
        [columns(keys, c, wide), core_in[part : part + tokens], id_tail], axis=0
    )
    k_line = [k_chunk] + [send(k_chunk, TO_Z[k]) for k in range(1, NZ)]
    k_across = [send(x, TO_Y) for x in k_line]
    k_chunks = k_line + k_across

    q_in = send(columns(queries, 1 - c, qwide), TO_CORE)
    q = jnp.concatenate([columns(queries, c, qwide), q_in], axis=0)

    low = jnp.dot(normed_hidden, adapter_down_weight, preferred_element_type=jnp.float32).astype(
        jnp.bfloat16
    )
    low_in = send(low, TO_CORE)
    adapter = 0.5 * jnp.dot(
        jnp.concatenate([low, low_in], axis=0),
        columns(adapter_up_weight, c, wide),
        preferred_element_type=jnp.float32,
    )

    chip_tokens = NCORE * tokens
    key_ids = jnp.stack([x[chip_tokens, : 2 * slots] for x in k_chunks]).astype(jnp.int32)
    offsets = jnp.arange(BLK, dtype=jnp.int32)
    kpos = (key_ids.reshape(-1, 1) * BLK + offsets[None, :]).reshape(1, -1)
    qid = key_ids[0]
    both = [weights_of(qid, q, kpos, k_chunks, chip_tokens, h) for h in range(KVH // NCORE)]

    def shard_list(ys):
        return jnp.stack(
            [
                ((z ^ k) * NY + ys) * NCORE + which
                for k in range(NZ)
                for which in (c, 1 - c)
            ]
        ).astype(jnp.int32)

    near, far = (x_mine, x_partner), (x_far, x_far_partner)
    line, across = shard_list(y), shard_list(1 - y)
    far_sum = value_product(line, far, w_line)
    near_sum = value_product(line, near, w_line)
    far_sum = value_product(across, far, w_across, far_sum)
    far_in = send(far_sum, TO_X)
    near_sum = value_product(across, near, w_across, near_sum)
    v_chunk = (near_sum + far_in + adapter).astype(jnp.bfloat16)
    v_line = [v_chunk] + [send(v_chunk, TO_Z[k]) for k in range(1, NZ)]
    v_across = [send(x, TO_Y) for x in v_line]

    ps = [x[0] for x in both]
    totals = [x[1] for x in both]
    sums = [first_sum(p, v_line, h) for h, p in enumerate(ps)]
    theirs = last_sum(ps, sums, totals, v_across, slots, slots)
    out_in = send(theirs, TO_CORE)
    ours = last_sum(ps, sums, totals, v_across, 0, slots)
    return jnp.where(
        c == 0,
        jnp.concatenate([ours, out_in], axis=1),
        jnp.concatenate([out_in, ours], axis=1),
    )


def solution(mesh):
    in_specs = (
        P(("group", "ctx"), None),
        P(("group", "ctx"), None),
        P(("group", "ctx"), None),
        P("ctx", None),
        P(),
        P(),
        P(("group", "ctx")),
    )
    out_specs = P(("group", "ctx"), None)
    fits = mesh.shape["group"] == PARTS and mesh.shape["ctx"] == CHIPS * NCORE
    step = chip_shards if fits else shards
    return jax.shard_map(step, mesh=mesh, in_specs=in_specs, out_specs=out_specs, check_vma=False)
```
